256 devices in a mesh: blk: 16 (over z, y_hi), dp: 16 (over y_lo, x, core).
Axes of the slice: x: 4, y: 4 (y_hi: 2, y_lo: 2; y = y_hi * 2 + y_lo), z: 8, core: 2. Of those that a mesh axis runs over, the one named last changes fastest.
Arguments:
- visual_rows: bfloat16 [16, 512, 4096], P('dp', 'blk'), may hold values from -6 to 6
- value_matrix: bfloat16 [16, 512, 512], P('dp', 'blk'), may hold values from -6 to 6
- key_weight: bfloat16 [4096, 512], replicated, may hold values from -1 to 1
- queries: bfloat16 [16, 2048, 4096], P('dp', 'blk'), may hold values from -1024 to 1024
- output_gradient: bfloat16 [16, 2048, 4096], P('dp', 'blk'), may hold values from -6 to 6
- visual_len: int32 [16], P('dp'), may hold values from 128 to 512, as said below
- frame_end: int32 [16, 16], P('dp'), may hold values from 1 to 4, as said below
Outputs:
- attn_out: bfloat16 [16, 2048, 4096], P('dp', 'blk')
- query_grad: bfloat16 [16, 2048, 4096], P('dp', 'blk')
- value_grad: bfloat16 [16, 512, 512], P('dp', 'blk')
- key_weight_grad: float32 [4096, 512], P(('blk', 'dp'))
The draws below stay inside these ranges and needn't reach their ends.
Inputs may be any that keep to these rules, and one draw needn't show every extreme that they name: `visual_len`: rows 0 to the count minus one of a sample are live; some sample has 512, another 128. `frame_end`: never falling along the text blocks of a sample, 1 for its first block and 4 for its last.
All inputs are finite; a program needn't handle non-finite values.
Results may differ from the reference program's by a relative error of at most 0.02.
Values may be sent and summed in bfloat16 or wider, within the bound.
A program may use at most 128 MiB of HBM per device.

```python
import math
import jax
import jax.numpy as jnp
from jax import lax

HQ = 32
KEY_HEADS = 4
HEAD_SIZE = 128
VISUAL_FEATURES = 4096
TILE = 128
HEADS_PER_KEY = 8
SAMPLE_COUNT = 16
TEXT_ROWS = 2048
VISUAL_ROWS = 512


def special_rows(key):
    drawn_sample = jax.random.normal(jax.random.fold_in(key, 101), (SAMPLE_COUNT, 2, VISUAL_FEATURES), jnp.float32)
    return jnp.clip(drawn_sample, -6.0, 6.0)


def key_matrix(key):
    drawn_sample = jax.random.normal(jax.random.fold_in(key, 102), (VISUAL_FEATURES, KEY_HEADS * HEAD_SIZE), jnp.float32)
    return jnp.clip(drawn_sample, -6.0, 6.0) / math.sqrt(VISUAL_FEATURES)


def draw_key_weight(key, part):
    return key_matrix(key).astype(jnp.bfloat16)


def draw_visual_rows(key, part):
    bulk = jnp.clip(jax.random.normal(jax.random.fold_in(key, 104), (SAMPLE_COUNT, VISUAL_ROWS, VISUAL_FEATURES), jnp.float32), -6.0, 6.0)
    bulk = bulk.at[:, 0:2, :].set(special_rows(key))
    return bulk.astype(jnp.bfloat16)


def draw_queries(key, part):
    base = 2.5 * jnp.clip(jax.random.normal(jax.random.fold_in(key, 106), (SAMPLE_COUNT, TEXT_ROWS, HQ * HEAD_SIZE), jnp.float32), -6.0, 6.0)
    return base.astype(jnp.bfloat16)


def draw_visual_len(key, part):
    lengths = jax.random.randint(jax.random.fold_in(key, 111), (SAMPLE_COUNT,), TILE, VISUAL_ROWS + 1)
    longest = jax.random.randint(jax.random.fold_in(key, 112), (), 0, SAMPLE_COUNT)
    shortest = (longest + jax.random.randint(jax.random.fold_in(key, 113), (), 1, SAMPLE_COUNT)) % SAMPLE_COUNT
    return lengths.at[longest].set(VISUAL_ROWS).at[shortest].set(TILE).astype(jnp.int32)


def draw_frame_end(key, part):
    steps_up = jax.random.randint(jax.random.fold_in(key, 121), (SAMPLE_COUNT, TEXT_ROWS // TILE), 1, 4)
    climb = jnp.cumsum(steps_up, axis=1)
    climb = climb - climb[:, :1]
    highest = climb[:, -1:]
    return (1 + climb * (VISUAL_ROWS // TILE - 1) // highest).astype(jnp.int32)


def block_levels(key, shape, pieces, smallest, largest):
    def one(axis_at, shards_of):
        steps = jax.random.uniform(jax.random.fold_in(jax.random.fold_in(key, 6), axis_at), (shards_of,), jnp.float32, smallest / len(pieces), largest / len(pieces))
        return jnp.repeat(jnp.exp(steps), shape[axis_at] // shards_of).reshape((-1,) + (1,) * (len(shape) - axis_at - 1))

    level = one(*pieces[0])
    for cut in pieces[1:]:
        level = level * one(*cut)
    return level


def scatter_about(key, shape, spread, bound, pieces=(), held_as=jnp.bfloat16):
    entries = spread * jax.random.normal(key, shape, jnp.float32)
    if pieces:
        entries = entries * block_levels(key, shape, pieces, -0.22, 0.18)
    return jnp.clip(entries, -bound, bound).astype(held_as)


def setup_inputs(seed: int = 0) -> dict:
    key_of = jax.random.split(jax.random.key(seed), 8)
    visual_rows = draw_visual_rows(jax.random.fold_in(key_of[7], 71), 0)
    value_matrix = scatter_about(key_of[1], (SAMPLE_COUNT, VISUAL_ROWS, KEY_HEADS * HEAD_SIZE), 1.0, 6.0, ((0, 16), (1, 16)))
    key_weight = draw_key_weight(jax.random.fold_in(key_of[7], 71), 0)
    queries = draw_queries(jax.random.fold_in(key_of[7], 71), 0)
    output_gradient = scatter_about(key_of[4], (SAMPLE_COUNT, TEXT_ROWS, HQ * HEAD_SIZE), 1.0, 6.0, ((0, 16), (1, 16)))
    visual_len = draw_visual_len(jax.random.fold_in(key_of[7], 71), 0)
    frame_end = draw_frame_end(jax.random.fold_in(key_of[7], 71), 0)
    return dict(visual_rows=visual_rows, value_matrix=value_matrix, key_weight=key_weight, queries=queries, output_gradient=output_gradient, visual_len=visual_len, frame_end=frame_end)


NEGATIVE_FILLER = -1.0e30


def one_sample(visual, value_single, key_weight, query_single, gradient_single, length, frames):
    head_span_width = KEY_HEADS * HEAD_SIZE
    scale = HEAD_SIZE ** -0.5
    key_rows = jnp.dot(visual, key_weight, preferred_element_type=jnp.float32).astype(jnp.bfloat16)
    limits = jnp.minimum(length, TILE * jnp.repeat(frames, TILE, total_repeat_length=TEXT_ROWS))
    live_mask = jnp.arange(VISUAL_ROWS, dtype=jnp.int32)[None, :] < limits[:, None]
    query_matrix = query_single.reshape(TEXT_ROWS, KEY_HEADS, HEADS_PER_KEY, HEAD_SIZE).astype(jnp.float32)
    gradient_rows = gradient_single.reshape(TEXT_ROWS, KEY_HEADS, HEADS_PER_KEY, HEAD_SIZE).astype(jnp.float32)
    key_portion = key_rows.reshape(VISUAL_ROWS, KEY_HEADS, HEAD_SIZE).astype(jnp.float32)
    value_portion = value_single.reshape(VISUAL_ROWS, KEY_HEADS, HEAD_SIZE).astype(jnp.float32)
    scores = jnp.einsum("tkgd,rkd->kgtr", query_matrix, key_portion) * scale
    scores = jnp.where(live_mask, scores, NEGATIVE_FILLER)
    row_peak = jnp.max(scores, axis=3, keepdims=True)
    shifted = jnp.where(live_mask, jnp.exp(scores - row_peak), 0.0)
    probs = shifted / jnp.sum(shifted, axis=3, keepdims=True)
    weights = lax.optimization_barrier(probs.astype(jnp.bfloat16)).astype(jnp.float32)
    attn_out = jnp.einsum("kgtr,rkd->tkgd", weights, value_portion).astype(jnp.bfloat16)
    out_wide = lax.optimization_barrier(attn_out).astype(jnp.float32)
    grad_delta = jnp.einsum("tkgd,tkgd->kgt", gradient_rows, out_wide)
    dprobs = jnp.einsum("tkgd,rkd->kgtr", gradient_rows, value_portion)
    dscores = (probs * (dprobs - grad_delta[..., None]) * scale).astype(jnp.bfloat16)
    dscores = lax.optimization_barrier(dscores).astype(jnp.float32)
    query_grad = jnp.einsum("kgtr,rkd->tkgd", dscores, key_portion).astype(jnp.bfloat16)
    key_grad = jnp.einsum("kgtr,tkgd->rkd", dscores, query_matrix).astype(jnp.bfloat16)
    value_grad = jnp.einsum("kgtr,tkgd->rkd", weights, gradient_rows).astype(jnp.bfloat16)
    weight_term = jnp.dot(visual.T, key_grad.reshape(VISUAL_ROWS, head_span_width), preferred_element_type=jnp.float32)
    return (attn_out.reshape(TEXT_ROWS, HQ * HEAD_SIZE), query_grad.reshape(TEXT_ROWS, HQ * HEAD_SIZE),
            value_grad.reshape(VISUAL_ROWS, head_span_width), weight_term)


def reference(visual_rows, value_matrix, key_weight, queries, output_gradient, visual_len, frame_end):
    def per_sample(total_grad, sample_slices):
        visual, value_single, query_single, gradient_single, length, frames = sample_slices
        attn_out, query_grad, value_grad, weight_term = one_sample(
            visual, value_single, key_weight, query_single, gradient_single, length, frames)
        return total_grad + weight_term, (attn_out, query_grad, value_grad)

    gradient_begin = jnp.zeros((VISUAL_FEATURES, KEY_HEADS * HEAD_SIZE), jnp.float32)
    weight_grad, (attn_out, query_grad, value_grad) = lax.scan(
        per_sample, gradient_begin, (visual_rows, value_matrix, queries, output_gradient, visual_len, frame_end))
    return attn_out, query_grad, value_grad, weight_grad
```

```python
import functools
import math

import jax
import jax.numpy as jnp
from jax import lax
from jax.experimental import pallas as pl
from jax.experimental.pallas import tpu as pltpu
from jax.sharding import PartitionSpec as P

HEADS = 4
GROUP = 8
D = 128
TILE = 128
ROWS = 32
SCALE = D ** (-0.5)
EXP2_SCALE = SCALE * math.log2(math.e)
FILLER = -1e30
MESH = pl.DeviceIdType.MESH
F32 = jnp.float32
BF16 = jnp.bfloat16
VM = pl.BlockSpec(memory_space=pltpu.VMEM)


def ring_position():
    b = lax.axis_index("blk")
    z, y = b // 2, b % 2
    nz = lax.axis_size("blk") // 2

    def at(step, yy):
        return lax.rem(z + step + nz, nz) * 2 + yy

    return b, z, y, nz, at


def copy_to(src, dst, send, recv, axis, index):
    c = pltpu.make_async_remote_copy(
        src_ref=src, dst_ref=dst, send_sem=send, recv_sem=recv,
        device_id={axis: index}, device_id_type=MESH)
    c.start()
    return c


class Gather:
    def __init__(self, bufs, send, recv, ysend, yrecv):
        self.bufs, self.send, self.recv = bufs, send, recv
        self.ysend, self.yrecv = ysend, yrecv
        self.b, self.z, self.y, self.nz, self.at = ring_position()
        self.copies = []
        self.ycopies = {}
        self.hops = {}

    def length(self, x, way):
        return self.nz // 2 if x == way else self.nz // 2 - 1

    def go(self, x, mine, way, hop):
        step = 1 if way == 0 else -1
        yy = self.y if mine == 0 else 1 - self.y
        slot = self.at(-step * (hop - 1), yy)
        ref = self.bufs[x].at[slot]
        c = copy_to(ref, ref, self.send.at[x, mine, way, hop - 1],
                    self.recv.at[x, mine, way, hop - 1], "blk", self.at(step, self.y))
        self.hops[x, mine, way, hop] = c
        self.copies.append(c)

    def start(self, x):
        ref = self.bufs[x].at[self.b]
        c = copy_to(ref, ref, self.ysend.at[x], self.yrecv.at[x], "blk", self.at(0, 1 - self.y))
        self.ycopies[x] = c
        self.copies.append(c)
        for way in (0, 1):
            self.go(x, 0, way, 1)

    def across(self, x):
        self.ycopies[x].wait_recv()
        for way in (0, 1):
            self.go(x, 1, way, 1)

    def advance(self, x, mine, hop):
        for way in (0, 1):
            n = self.length(x, way)
            if hop <= n:
                self.hops[x, mine, way, hop].wait_recv()
                if hop < n:
                    self.go(x, mine, way, hop + 1)

    def run(self):
        for hop in range(1, self.nz // 2 + 1):
            for x in (0, 1):
                self.advance(x, 0, hop)
                if hop == 1:
                    self.across(x)
            for x in (0, 1):
                self.advance(x, 1, hop)

    def finish(self):
        for c in self.copies:
            c.wait_send()


class Scatter:
    def __init__(self, parts, inbox, outbox, yin, yout, send, recv, ysend, yrecv):
        self.parts, self.inbox, self.outbox = parts, inbox, outbox
        self.yin, self.yout = yin, yout
        self.send, self.recv, self.ysend, self.yrecv = send, recv, ysend, yrecv
        self.b, self.z, self.y, self.nz, self.at = ring_position()
        self.copies = []
        self.hops = {}

    def length(self, x, way):
        return self.nz // 2 if x == way else self.nz // 2 - 1

    def go(self, x, way, hop):
        step = 1 if way == 0 else -1
        n = self.length(x, way)
        first = self.at(step * (n - hop + 1), 0)
        rows = self.parts[x].at[pl.ds(first, 2)]
        if hop == 1:
            src = rows
        else:
            src = self.outbox.at[x, way, hop - 2]
            src[...] = (rows[...].astype(F32) + self.inbox[x, way, hop - 2].astype(F32)).astype(BF16)
        c = copy_to(src, self.inbox.at[x, way, hop - 1], self.send.at[x, way, hop - 1],
                    self.recv.at[x, way, hop - 1], "blk", self.at(step, self.y))
        self.hops[x, way, hop] = c
        self.copies.append(c)

    def start(self, x):
        for way in (0, 1):
            self.go(x, way, 1)

    def advance(self, x, hop):
        for way in (0, 1):
            n = self.length(x, way)
            if hop <= n:
                self.hops[x, way, hop].wait_recv()
                if hop < n:
                    self.go(x, way, hop + 1)

    def sum_at(self, x, slot, yy):
        total = self.parts[x][slot].astype(F32)
        for way in (0, 1):
            total += self.inbox[x, way, self.length(x, way) - 1, yy].astype(F32)
        return total

    def across(self, x):
        other = 1 - self.y
        self.yout[x] = self.sum_at(x, self.at(0, other), other).astype(BF16)
        c = copy_to(self.yout.at[x], self.yin.at[x], self.ysend.at[x], self.yrecv.at[x],
                    "blk", self.at(0, other))
        self.copies.append(c)
        return c

    def run(self):
        for x in (0, 1):
            self.start(x)
        for hop in range(1, self.nz // 2 + 1):
            for x in (0, 1):
                self.advance(x, hop)
        return [self.across(x) for x in (0, 1)]

    def result(self, x, c):
        c.wait_recv()
        return self.sum_at(x, self.b, self.y) + self.yin[x].astype(F32)

    def finish(self):
        for c in self.copies:
            c.wait_send()


def greet(axis_peers):
    barrier = pltpu.get_barrier_semaphore()
    for axis, index in axis_peers:
        pl.semaphore_signal(barrier, inc=1, device_id={axis: index}, device_id_type=MESH)
    return lambda: pl.semaphore_wait(barrier, len(axis_peers))


def others(axis):
    n = lax.axis_size(axis)
    me = lax.axis_index(axis)
    return [(i, lax.rem(me + i, n)) for i in range(1, n)]


def gather_kernel(visual, values, weight, k_out, v_out, vis_out,
                  send, recv, ysend, yrecv, vsend, vrecv, local):
    b = lax.axis_index("blk")
    n = lax.axis_size("blk")
    width = visual.shape[1] // n
    ready = greet([("blk", j) for _, j in others("blk")])
    g = Gather((v_out, k_out), send, recv, ysend, yrecv)
    v_out[b] = values[...]
    k_out[b] = jnp.dot(visual[...], weight[...], preferred_element_type=F32).astype(BF16)
    ready()
    g.start(0)
    g.start(1)
    own = pltpu.make_async_copy(
        visual.at[:, pl.ds(pl.multiple_of(b * width, width), width)], vis_out.at[b], local)
    own.start()
    moves = []
    for i, j in others("blk"):
        moves.append(copy_to(
            visual.at[:, pl.ds(pl.multiple_of(j * width, width), width)], vis_out.at[b],
            vsend.at[i - 1], vrecv.at[i - 1], "blk", j))
    g.run()
    g.finish()
    own.wait()
    for c in moves:
        c.wait_send()
        c.wait_recv()


def dot(a, b, dims):
    return lax.dot_general(a, b, (dims, ((), ())), preferred_element_type=F32)


def attention_kernel(length, frames, q_ref, g_ref, k_ref, v_ref, o_ref, dq_ref, dk_ref, dv_ref):
    tile = lax.axis_index("blk")
    limit = jnp.minimum(length[0], TILE * frames[0, tile])
    k, v = k_ref[...], v_ref[...]
    k_t, v_t = k.T, v.T
    rows = k.shape[0]
    dk = dv = None
    for p in range(GROUP // 2):
        at = [slice((2 * p + i) * D, (2 * p + i + 1) * D) for i in (0, 1)]
        q = jnp.concatenate([q_ref[:, s] for s in at], axis=0)
        g = jnp.concatenate([g_ref[:, s] for s in at], axis=0)
        g_t = g.T
        s = dot(k, q, ((1,), (1,)))
        live = lax.broadcasted_iota(jnp.int32, s.shape, 0) < limit
        s = jnp.where(live, s, FILLER)
        peak = jnp.max(s, axis=0, keepdims=True)
        e = jnp.exp2((s - peak) * EXP2_SCALE)
        probs = e * (1.0 / jnp.sum(e, axis=0, keepdims=True))
        w = probs.astype(BF16)
        o_t = dot(v_t, w, ((1,), (0,))).astype(BF16).astype(F32)
        delta = jnp.sum(g_t.astype(F32) * o_t, axis=0, keepdims=True)
        dp = dot(v, g_t, ((1,), (0,)))
        ds = (probs * ((dp - delta) * SCALE)).astype(BF16)
        dq_t = dot(k_t, ds, ((1,), (0,)))
        o = o_t.T.astype(BF16)
        dq = dq_t.T.astype(BF16)
        for i in (0, 1):
            o_ref[:, at[i]] = o[i * D:(i + 1) * D]
            dq_ref[:, at[i]] = dq[i * D:(i + 1) * D]
        dv_p = dot(w, g, ((1,), (0,)))
        dk_p = dot(ds, q, ((1,), (0,)))
        dv = dv_p if dv is None else dv + dv_p
        dk = dk_p if dk is None else dk + dk_p
    dk_ref[...] = dk.astype(BF16)
    dv_ref[...] = dv.astype(BF16)


def reduce_kernel(dk, dv, vis, dv_out, dw_out,
                  inbox, outbox, yin, yout, kg0, kg1, part, landed,
                  send, recv, ysend, yrecv, gsend, grecv, gysend, gyrecv, wsend, wrecv):
    b, z, y, nz, at = ring_position()
    d = lax.axis_index("dp")
    n = lax.axis_size("dp")
    ready = greet([("blk", at(1, y)), ("blk", at(-1, y)), ("blk", at(0, 1 - y))]
                  + [("dp", j) for _, j in others("dp")])
    ready()
    r = Scatter((dk, dv), inbox, outbox, yin, yout, send, recv, ysend, yrecv)
    ck, cv = r.run()
    key_grad = r.result(0, ck).astype(BF16)
    half = key_grad.shape[1] // 2
    g = Gather((kg0, kg1), gsend, grecv, gysend, gyrecv)
    kg0[b] = key_grad[:, :half]
    g.start(0)
    kg1[b] = key_grad[:, half:]
    g.start(1)
    dv_out[...] = r.result(1, cv).astype(BF16)
    vis_t = vis[...].reshape(-1, vis.shape[2]).T
    g.run()
    for i, kg in enumerate((kg0, kg1)):
        w = dot(vis_t, kg[...].reshape(-1, half), ((1,), (0,)))
        part[:, :, i * half:(i + 1) * half] = w.astype(BF16).reshape(n, -1, half)
    moves = []
    for i, j in others("dp"):
        moves.append(copy_to(part.at[j], landed.at[i - 1], wsend.at[i - 1], wrecv.at[i - 1], "dp", j))
    total = part[d].astype(F32)
    for i, c in enumerate(moves):
        c.wait_recv()
        total += landed[i].astype(F32)
    dw_out[...] = total
    r.finish()
    g.finish()
    for c in moves:
        c.wait_send()


def local(visual_rows, value_matrix, key_weight, queries, output_gradient, visual_len, frame_end):
    nb, nd = lax.axis_size("blk"), lax.axis_size("dp")
    hop = nb // 4
    width = HEADS * D
    features = visual_rows.shape[2]
    per = features // nb
    text = queries.shape[1]
    dma = pltpu.SemaphoreType.DMA
    gather_sems = [dma((2, 2, 2, hop)), dma((2, 2, 2, hop)), dma((2,)), dma((2,))]

    keys, values, vis = pl.pallas_call(
        gather_kernel,
        out_shape=(
            jax.ShapeDtypeStruct((nb, ROWS, width), BF16),
            jax.ShapeDtypeStruct((nb, ROWS, width), BF16),
            jax.ShapeDtypeStruct((nb, ROWS, per), BF16),
        ),
        in_specs=[VM] * 3,
        out_specs=(VM,) * 3,
        scratch_shapes=gather_sems + [dma((nb - 1,)), dma((nb - 1,)), dma],
        compiler_params=pltpu.CompilerParams(collective_id=0, has_side_effects=True),
        name="gather_rows",
    )(visual_rows[0], value_matrix[0], key_weight)

    total = nb * ROWS
    col = lambda rows, c: pl.BlockSpec((rows, c), lambda i: (0, i))
    smem = pl.BlockSpec(memory_space=pltpu.SMEM)
    attn_out, query_grad, dk, dv = pl.pallas_call(
        attention_kernel,
        grid=(HEADS,),
        out_shape=(
            jax.ShapeDtypeStruct((text, queries.shape[2]), BF16),
            jax.ShapeDtypeStruct((text, queries.shape[2]), BF16),
            jax.ShapeDtypeStruct((total, width), BF16),
            jax.ShapeDtypeStruct((total, width), BF16),
        ),
        in_specs=[smem, smem, col(text, GROUP * D), col(text, GROUP * D), col(total, D), col(total, D)],
        out_specs=(col(text, GROUP * D), col(text, GROUP * D), col(total, D), col(total, D)),
        compiler_params=pltpu.CompilerParams(vmem_limit_bytes=48 << 20),
        name="attention",
    )(visual_len, frame_end, queries[0], output_gradient[0],
      keys.reshape(total, width), values.reshape(total, width))

    value_grad, weight_grad = pl.pallas_call(
        reduce_kernel,
        out_shape=(
            jax.ShapeDtypeStruct((ROWS, width), BF16),
            jax.ShapeDtypeStruct((per // nd, width), F32),
        ),
        in_specs=[VM] * 3,
        out_specs=(VM,) * 2,
        scratch_shapes=[
            pltpu.VMEM((2, 2, hop, 2, ROWS, width), BF16),
            pltpu.VMEM((2, 2, hop - 1, 2, ROWS, width), BF16),
            pltpu.VMEM((2, ROWS, width), BF16),
            pltpu.VMEM((2, ROWS, width), BF16),
            pltpu.VMEM((nb, ROWS, width // 2), BF16),
            pltpu.VMEM((nb, ROWS, width // 2), BF16),
            pltpu.VMEM((nd, per // nd, width), BF16),
            pltpu.VMEM((nd - 1, per // nd, width), BF16),
            dma((2, 2, hop)), dma((2, 2, hop)), dma((2,)), dma((2,)),
        ] + gather_sems + [dma((nd - 1,)), dma((nd - 1,))],
        compiler_params=pltpu.CompilerParams(collective_id=1, has_side_effects=True),
        name="reduce_rows",
    )(dk.reshape(nb, ROWS, width), dv.reshape(nb, ROWS, width), vis)
    return attn_out[None], query_grad[None], value_grad[None], weight_grad


def solution(mesh):
    return jax.shard_map(
        local,
        mesh=mesh,
        in_specs=(
            P("dp", "blk", None),
            P("dp", "blk", None),
            P(),
            P("dp", "blk", None),
            P("dp", "blk", None),
            P("dp"),
            P("dp", None),
        ),
        out_specs=(
            P("dp", "blk", None),
            P("dp", "blk", None),
            P("dp", "blk", None),
            P(("blk", "dp"), None),
        ),
        check_vma=False,
    )
```

```python
import math

import jax
import jax.numpy as jnp
from jax import lax
from jax.experimental import pallas as pl
from jax.experimental.pallas import tpu as pltpu
from jax.sharding import PartitionSpec as P

HEADS = 4
GROUP = 8
D = 128
SPAN = GROUP * D
TILE = 128
ROWS = 32
SCALE = D ** (-0.5)
EXP2_SCALE = SCALE * math.log2(math.e)
FILLER = -1e30
MESH = pl.DeviceIdType.MESH
F32 = jnp.float32
BF16 = jnp.bfloat16


def dot(a, b, dims):
    return lax.dot_general(a, b, (dims, ((), ())), preferred_element_type=F32)


def near_first(n):
    return sorted(range(1, n), key=lambda i: min(i, n - i))


def kernel(length, frames, visual_hbm, values_hbm, weight_hbm, queries_hbm, grads_hbm,
           o_hbm, dq_hbm, dv_out, dw_out,
           visual, values, weight, q_ref, g_ref, o_ref, dq_ref, bias,
           kv, part, yin, half, zin, kg, vis, wpart, landed,
           load, weight_load, store,
           zsend, zrecv, fsend, frecv, vsend, vrecv,
           ysend, yrecv, hsend, hrecv, ksend, krecv, wsend, wrecv):
    b = lax.axis_index("blk")
    d = lax.axis_index("dp")
    nb, nd = lax.axis_size("blk"), lax.axis_size("dp")
    nz = nb // 2
    z, y = b // 2, b % 2
    per = visual.shape[1] // nb

    def zmod(i):
        return lax.rem(z + i, nz)

    def zpeer(i):
        return zmod(i) * 2 + y

    partner = b + 1 - 2 * y
    peers = [(i, s) for i in [0] + near_first(nz) for s in (0, 1) if i or s]
    sent = []

    def send(src, dst, ssem, rsem, axis, index):
        c = pltpu.make_async_remote_copy(
            src_ref=src, dst_ref=dst, send_sem=ssem, recv_sem=rsem,
            device_id={axis: index}, device_id_type=MESH)
        c.start()
        sent.append(c)
        return c

    def side(s):
        return y if s == 0 else 1 - y

    def at(i, s):
        return zmod(i) * 2 + side(s)

    loads = []
    for i, (src, dst) in enumerate(((visual_hbm, visual), (values_hbm, values))):
        loads.append(pltpu.make_async_copy(src, dst, load.at[i]))
        loads[-1].start()
    wloads = []
    for j in range(HEADS):
        cols = pl.ds(j * D, D)
        wloads.append(pltpu.make_async_copy(weight_hbm.at[:, cols], weight.at[:, cols], weight_load.at[j]))
        wloads[-1].start()
    for i, (src, dst) in enumerate(((queries_hbm, q_ref), (grads_hbm, g_ref))):
        loads.append(pltpu.make_async_copy(src, dst, load.at[2 + i]))
        loads[-1].start()

    barrier = pltpu.get_barrier_semaphore()
    for i, s in peers:
        pl.semaphore_signal(barrier, inc=1, device_id={"blk": at(i, s)}, device_id_type=MESH)
    for i in range(1, nd):
        pl.semaphore_signal(barrier, inc=1, device_id={"dp": lax.rem(d + i, nd)}, device_id_type=MESH)

    limit = jnp.minimum(length[0], TILE * frames[0, b])
    r = lax.broadcasted_iota(jnp.int32, bias.shape, 0)
    row = ((r & (nz * ROWS - 1)) // ROWS) * (2 * ROWS) + (r // (nz * ROWS)) * ROWS + (r & (ROWS - 1))
    bias[...] = jnp.where(row < limit, 0.0, FILLER)

    zcopies, fcopies = {}, {}

    def project(j):
        wloads[j].wait()
        cols = slice(j * D, (j + 1) * D)
        key = jnp.dot(visual[...], weight[:, cols], preferred_element_type=F32)
        kv[j, y, z, :, :D] = key.astype(BF16)
        kv[j, y, z, :, D:] = values[:, cols]

    def gather(j):
        ref = kv.at[j, y, z]
        fcopies[j, 0] = send(ref, ref, fsend.at[j, 0], frecv.at[j, 0], "blk", partner)
        for i in near_first(nz):
            zcopies[j, i] = send(ref, ref, zsend.at[j, i - 1], zrecv.at[j, i - 1], "blk", zpeer(i))

    def forward(j):
        for i in near_first(nz):
            zcopies[j, i].wait_recv()
            ref = kv.at[j, y, zmod(nz - i)]
            fcopies[j, i] = send(ref, ref, fsend.at[j, i], frecv.at[j, i], "blk", partner)

    def arrive(j):
        for i in range(nz):
            fcopies[j, i].wait_recv()

    vcopies = []

    def exchange():
        for n, (i, s) in enumerate(peers):
            t = at(i, s)
            vcopies.append(send(
                visual.at[:, pl.ds(pl.multiple_of(t * per, per), per)], vis.at[y, z],
                vsend.at[n], vrecv.at[n], "blk", t))
        vis[y, z] = visual[:, pl.ds(pl.multiple_of(b * per, per), per)]

    stores = []

    def attention(j):
        block = kv[j].reshape(nb * ROWS, 2 * D)
        k, v = block[:, :D], block[:, D:]
        k_t, v_t = k.T, v.T
        dk = dv = None
        for p in range(GROUP // 2):
            cols = [slice(j * SPAN + (2 * p + i) * D, j * SPAN + (2 * p + i + 1) * D) for i in (0, 1)]
            q = jnp.concatenate([q_ref[:, c] for c in cols], axis=0)
            g = jnp.concatenate([g_ref[:, c] for c in cols], axis=0)
            g_t = g.T
            s = dot(k, q, ((1,), (1,))) + bias[...]
            peak = jnp.max(s, axis=0, keepdims=True)
            e = jnp.exp2((s - peak) * EXP2_SCALE)
            probs = e * (1.0 / jnp.sum(e, axis=0, keepdims=True))
            w = probs.astype(BF16)
            o_t = dot(v_t, w, ((1,), (0,))).astype(BF16).astype(F32)
            delta = jnp.sum(g_t.astype(F32) * o_t, axis=0, keepdims=True)
            dp = dot(v, g_t, ((1,), (0,)))
            ds = (probs * ((dp - delta) * SCALE)).astype(BF16)
            dq_t = dot(k_t, ds, ((1,), (0,)))
            o = o_t.T.astype(BF16)
            dq = dq_t.T.astype(BF16)
            for i in (0, 1):
                o_ref[:, cols[i]] = o[i * D:(i + 1) * D]
                dq_ref[:, cols[i]] = dq[i * D:(i + 1) * D]
            dv_p = dot(w, g, ((1,), (0,)))
            dk_p = dot(ds, q, ((1,), (0,)))
            dv = dv_p if dv is None else dv + dv_p
            dk = dk_p if dk is None else dk + dk_p
        part[j, :, :, :, :D] = dk.astype(BF16).reshape(2, nz, ROWS, D)
        part[j, :, :, :, D:] = dv.astype(BF16).reshape(2, nz, ROWS, D)
        cols = pl.ds(j * SPAN, SPAN)
        for i, (src, dst) in enumerate(((o_ref, o_hbm), (dq_ref, dq_hbm))):
            c = pltpu.make_async_copy(src.at[:, cols], dst.at[:, cols], store.at[i, j])
            c.start()
            stores.append(c)

    ycopies, hcopies, kcopies, wcopies = {}, {}, {}, {}

    def swap(j):
        ycopies[j] = send(part.at[j, 1 - y], yin.at[j], ysend.at[j], yrecv.at[j], "blk", partner)

    def scatter(j):
        ycopies[j].wait_recv()
        half[j] = (part[j, y].astype(F32) + yin[j].astype(F32)).astype(BF16)
        for i in near_first(nz):
            hcopies[j, i] = send(half.at[j, zmod(i)], zin.at[j, i - 1],
                                 hsend.at[j, i - 1], hrecv.at[j, i - 1], "blk", zpeer(i))

    def collect(j):
        total = half[j, z].astype(F32)
        for i in near_first(nz):
            hcopies[j, i].wait_recv()
            total += zin[j, i - 1].astype(F32)
        kg[j, y, z] = total[:, :D].astype(BF16)
        ref = kg.at[j, y, z]
        for n, (i, s) in enumerate(peers):
            kcopies[j, n] = send(ref, ref, ksend.at[j, n], krecv.at[j, n], "blk", at(i, s))
        dv_out[:, j * D:(j + 1) * D] = total[:, D:].astype(BF16)

    def weight_term(j, vis_t):
        for n in range(len(peers)):
            kcopies[j, n].wait_recv()
        term = dot(vis_t, kg[j].reshape(nb * ROWS, D), ((1,), (0,)))
        wpart[j] = term.astype(BF16).reshape(nd, per // nd, D)
        for i in range(1, nd):
            t = lax.rem(d + i, nd)
            wcopies[j, i] = send(wpart.at[j, t], landed.at[j, i - 1],
                                 wsend.at[j, i - 1], wrecv.at[j, i - 1], "dp", t)

    def weight_sum(j):
        total = wpart[j, d].astype(F32)
        for i in range(1, nd):
            wcopies[j, i].wait_recv()
            total += landed[j, i - 1].astype(F32)
        dw_out[:, j * D:(j + 1) * D] = total

    loads[0].wait()
    loads[1].wait()
    project(0)
    pl.semaphore_wait(barrier, len(peers) + nd - 1)
    gather(0)
    for j in range(1, HEADS):
        project(j)
        gather(j)
    forward(0)
    forward(1)
    loads[2].wait()
    loads[3].wait()
    arrive(0)
    attention(0)
    swap(0)
    forward(2)
    forward(3)
    exchange()
    arrive(1)
    attention(1)
    swap(1)
    scatter(0)
    arrive(2)
    attention(2)
    swap(2)
    scatter(1)
    collect(0)
    arrive(3)
    attention(3)
    swap(3)
    scatter(2)
    collect(1)
    for c in vcopies:
        c.wait_recv()
    vis_t = vis[...].reshape(nb * ROWS, per).T
    weight_term(0, vis_t)
    scatter(3)
    collect(2)
    weight_term(1, vis_t)
    collect(3)
    weight_term(2, vis_t)
    weight_sum(0)
    weight_sum(1)
    weight_term(3, vis_t)
    weight_sum(2)
    weight_sum(3)
    for c in sent:
        c.wait_send()
    for c in stores:
        c.wait()


def local(visual_rows, value_matrix, key_weight, queries, output_gradient, visual_len, frame_end):
    nb, nd = lax.axis_size("blk"), lax.axis_size("dp")
    nz = nb // 2
    width = HEADS * D
    features = visual_rows.shape[2]
    per = features // nb
    text = queries.shape[1]
    columns = queries.shape[2]
    dma = pltpu.SemaphoreType.DMA
    smem = pl.BlockSpec(memory_space=pltpu.SMEM)
    vmem = pl.BlockSpec(memory_space=pltpu.VMEM)
    hbm = pl.BlockSpec(memory_space=pl.ANY)

    def pair(*shape):
        return [dma(shape), dma(shape)]

    attn_out, query_grad, value_grad, weight_grad = pl.pallas_call(
        kernel,
        out_shape=(
            jax.ShapeDtypeStruct((text, columns), BF16),
            jax.ShapeDtypeStruct((text, columns), BF16),
            jax.ShapeDtypeStruct((ROWS, width), BF16),
            jax.ShapeDtypeStruct((per // nd, width), F32),
        ),
        in_specs=[smem] * 2 + [hbm] * 5,
        out_specs=(hbm, hbm, vmem, vmem),
        scratch_shapes=[
            pltpu.VMEM((ROWS, features), BF16),
            pltpu.VMEM((ROWS, width), BF16),
            pltpu.VMEM((features, width), BF16),
            pltpu.VMEM((text, columns), BF16),
            pltpu.VMEM((text, columns), BF16),
            pltpu.VMEM((text, columns), BF16),
            pltpu.VMEM((text, columns), BF16),
            pltpu.VMEM((nb * ROWS, 2 * D), F32),
            pltpu.VMEM((HEADS, 2, nz, ROWS, 2 * D), BF16),
            pltpu.VMEM((HEADS, 2, nz, ROWS, 2 * D), BF16),
            pltpu.VMEM((HEADS, nz, ROWS, 2 * D), BF16),
            pltpu.VMEM((HEADS, nz, ROWS, 2 * D), BF16),
            pltpu.VMEM((HEADS, nz - 1, ROWS, 2 * D), BF16),
            pltpu.VMEM((HEADS, 2, nz, ROWS, D), BF16),
            pltpu.VMEM((2, nz, ROWS, per), BF16),
            pltpu.VMEM((HEADS, nd, per // nd, D), BF16),
            pltpu.VMEM((HEADS, nd - 1, per // nd, D), BF16),
            dma((4,)), dma((HEADS,)), dma((2, HEADS)),
            *pair(HEADS, nz - 1), *pair(HEADS, nz), *pair(nb - 1),
            *pair(HEADS), *pair(HEADS, nz - 1), *pair(HEADS, nb - 1), *pair(HEADS, nd - 1),
        ],
        compiler_params=pltpu.CompilerParams(
            collective_id=0, has_side_effects=True, vmem_limit_bytes=56 << 20),
        name="cross_attention",
    )(visual_len, frame_end, visual_rows[0], value_matrix[0], key_weight, queries[0], output_gradient[0])
    return attn_out[None], query_grad[None], value_grad[None], weight_grad


def solution(mesh):
    return jax.shard_map(
        local,
        mesh=mesh,
        in_specs=(
            P("dp", "blk", None),
            P("dp", "blk", None),
            P(),
            P("dp", "blk", None),
            P("dp", "blk", None),
            P("dp"),
            P("dp", None),
        ),
        out_specs=(
            P("dp", "blk", None),
            P("dp", "blk", None),
            P("dp", "blk", None),
            P(("blk", "dp"), None),
        ),
        check_vma=False,
    )
```

```python
import math

import jax
import jax.numpy as jnp
from jax import lax
from jax.experimental import pallas as pl
from jax.experimental.pallas import tpu as pltpu
from jax.sharding import PartitionSpec as P

HEADS = 4
GROUP = 8
D = 128
SPAN = GROUP * D
TILE = 128
ROWS = 32
SCALE = D ** (-0.5)
EXP2_SCALE = SCALE * math.log2(math.e)
FILLER = -1e30
MESH = pl.DeviceIdType.MESH
F32 = jnp.float32
BF16 = jnp.bfloat16


def dot(a, b, dims):
    return lax.dot_general(a, b, (dims, ((), ())), preferred_element_type=F32)


def near_first(n):
    return sorted(range(1, n), key=lambda i: min(i, n - i))


def kernel(length, frames, visual_hbm, values_hbm, weight_hbm, queries_hbm, grads_hbm,
           o_ref, dq_ref, dv_out, dw_out,
           visual, values, weight, q_ref, g_ref, bias,
           kv, w_all, ds_all, o_all, part, yin, half, zin, direct, vpart, vyin, vhalf, vzin,
           kg, vis, wpart, landed,
           load, weight_load, out_sem, zrecv, frecv, vrecv,
           yrecv, hrecv, drecv, vyrecv, vhrecv, krecv, wrecv):
    b = lax.axis_index("blk")
    d = lax.axis_index("dp")
    nb, nd = lax.axis_size("blk"), lax.axis_size("dp")
    nz = nb // 2
    z, y = b // 2, b % 2
    per = visual.shape[1] // nb

    def zmod(i):
        return lax.rem(z + i, nz)

    def zpeer(i):
        return zmod(i) * 2 + y

    partner = b + 1 - 2 * y
    peers = [(i, s) for i in [0] + near_first(nz) for s in (0, 1) if i or s]
    sent = []

    def send(src, dst, rsem, axis, index):
        c = pltpu.make_async_remote_copy(
            src_ref=src, dst_ref=dst, send_sem=out_sem, recv_sem=rsem,
            device_id={axis: index}, device_id_type=MESH)
        c.start()
        sent.append(math.prod(src.shape))
        return c

    def wait_for(sem, elements):
        width = weight.shape[1] if elements % (16 * weight.shape[1]) == 0 else D
        ref = weight.at[pl.ds(0, elements // width), pl.ds(0, width)]
        pltpu.make_async_copy(ref, ref, sem).wait()

    def side(s):
        return y if s == 0 else 1 - y

    def at(i, s):
        return zmod(i) * 2 + side(s)

    loads = []
    for i, (src, dst) in enumerate(((visual_hbm, visual), (values_hbm, values))):
        loads.append(pltpu.make_async_copy(src, dst, load.at[i]))
        loads[-1].start()
    wloads = []
    for j in range(HEADS):
        cols = pl.ds(j * D, D)
        wloads.append(pltpu.make_async_copy(weight_hbm.at[:, cols], weight.at[:, cols], weight_load.at[j]))
        wloads[-1].start()
    for i, (src, dst) in enumerate(((queries_hbm, q_ref), (grads_hbm, g_ref))):
        loads.append(pltpu.make_async_copy(src, dst, load.at[2 + i]))
        loads[-1].start()

    barrier = pltpu.get_barrier_semaphore()
    line = [zpeer(i) for i in range(1, nz)] + [partner]
    for t in line:
        pl.semaphore_signal(barrier, inc=1, device_id={"blk": t}, device_id_type=MESH)
    for i in range(1, nd):
        pl.semaphore_signal(barrier, inc=1, device_id={"dp": lax.rem(d + i, nd)}, device_id_type=MESH)

    limit = jnp.minimum(length[0], TILE * frames[0, b])
    r = lax.broadcasted_iota(jnp.int32, bias.shape, 0)
    row = ((r & (nz * ROWS - 1)) // ROWS) * (2 * ROWS) + (r // (nz * ROWS)) * ROWS + (r & (ROWS - 1))
    bias[...] = jnp.where(row < limit, 0.0, FILLER)

    zcopies, fcopies = {}, {}

    def project(j):
        wloads[j].wait()
        cols = slice(j * D, (j + 1) * D)
        key = jnp.dot(visual[...], weight[:, cols], preferred_element_type=F32)
        kv[j, y, z, :, :D] = key.astype(BF16)
        kv[j, y, z, :, D:] = values[:, cols]

    def gather(j):
        ref = kv.at[j, y, z]
        fcopies[j, 0] = send(ref, ref, frecv.at[j], "blk", partner)
        for i in near_first(nz):
            zcopies[j, i] = send(ref, ref, zrecv.at[j, i - 1], "blk", zpeer(i))

    def forward(j):
        for i in near_first(nz):
            zcopies[j, i].wait_recv()
            ref = kv.at[j, y, zmod(nz - i)]
            fcopies[j, i] = send(ref, ref, frecv.at[j], "blk", partner)

    def arrive(j):
        wait_for(frecv.at[j], nz * ROWS * 2 * D)

    def exchange():
        for i, s in peers:
            t = at(i, s)
            send(visual.at[:, pl.ds(pl.multiple_of(t * per, per), per)], vis.at[y, z], vrecv, "blk", t)
        vis[y, z] = visual[:, pl.ds(pl.multiple_of(b * per, per), per)]

    def stack(ref, j, first, count):
        at0 = j * SPAN + first * D
        return jnp.concatenate([ref[:, at0 + i * D:at0 + (i + 1) * D] for i in range(count)], axis=0)

    def rows_of(j):
        block = kv[j].reshape(nb * ROWS, 2 * D)
        return block[:, :D], block[:, D:]

    def attention(j):
        k, v = rows_of(j)
        v_t = v.T
        for p in range(GROUP // 2):
            cols = slice(2 * p * D, (2 * p + 2) * D)
            q = stack(q_ref, j, 2 * p, 2)
            g_t = stack(g_ref, j, 2 * p, 2).T
            s = dot(k, q, ((1,), (1,))) + bias[...]
            peak = jnp.max(s, axis=0, keepdims=True)
            e = jnp.exp2((s - peak) * EXP2_SCALE)
            probs = e * (1.0 / jnp.sum(e, axis=0, keepdims=True))
            w = probs.astype(BF16)
            w_all[j, :, cols] = w
            o_t = dot(v_t, w, ((1,), (0,))).astype(BF16)
            o_all[j, :, cols] = o_t
            delta = jnp.sum(g_t.astype(F32) * o_t.astype(F32), axis=0, keepdims=True)
            dp = dot(v, g_t, ((1,), (0,)))
            ds_all[j, :, cols] = (probs * ((dp - delta) * SCALE)).astype(BF16)
        dk = dot(ds_all[j], stack(q_ref, j, 0, GROUP), ((1,), (0,)))
        part[j] = dk.astype(BF16).reshape(2, nz, ROWS, D)

    def finish(j):
        k, _ = rows_of(j)
        dv = dot(w_all[j], stack(g_ref, j, 0, GROUP), ((1,), (0,)))
        vpart[j // 2, :, :, :, (j % 2) * D:(j % 2 + 1) * D] = dv.astype(BF16).reshape(2, nz, ROWS, D)
        dq_t = dot(k.T, ds_all[j], ((1,), (0,)))
        for i in range(GROUP):
            cols = slice(j * SPAN + i * D, j * SPAN + (i + 1) * D)
            o_ref[:, cols] = o_all[j, :, i * D:(i + 1) * D].T
            dq_ref[:, cols] = dq_t[:, i * D:(i + 1) * D].T.astype(BF16)

    def swap(j):
        send(part.at[j, 1 - y], yin.at[j], yrecv.at[j], "blk", partner)

    def scatter(j):
        wait_for(yrecv.at[j], nz * ROWS * D)
        half[j] = (part[j, y].astype(F32) + yin[j].astype(F32)).astype(BF16)
        for i in near_first(nz):
            send(half.at[j, zmod(i)], zin.at[j, i - 1], hrecv.at[j], "blk", zpeer(i))

    def publish(j, total):
        kg[j, y, z] = total.astype(BF16)
        ref = kg.at[j, y, z]
        for i, s in peers:
            send(ref, ref, krecv.at[j], "blk", at(i, s))

    def collect(j):
        wait_for(hrecv.at[j], (nz - 1) * ROWS * D)
        total = half[j, z].astype(F32)
        for i in range(1, nz):
            total += zin[j, i - 1].astype(F32)
        publish(j, total)

    def spread(j):
        for n, (i, s) in enumerate(peers):
            send(part.at[j, side(s), zmod(i)], direct.at[n], drecv, "blk", at(i, s))

    def collect_direct(j):
        wait_for(drecv, len(peers) * ROWS * D)
        total = part[j, y, z].astype(F32)
        for n in range(len(peers)):
            total += direct[n].astype(F32)
        publish(j, total)

    def vswap(h):
        send(vpart.at[h, 1 - y], vyin.at[h], vyrecv.at[h], "blk", partner)

    def vscatter(h):
        wait_for(vyrecv.at[h], nz * ROWS * 2 * D)
        vhalf[h] = (vpart[h, y].astype(F32) + vyin[h].astype(F32)).astype(BF16)
        for i in near_first(nz):
            send(vhalf.at[h, zmod(i)], vzin.at[h, i - 1], vhrecv.at[h], "blk", zpeer(i))

    def vcollect(h):
        wait_for(vhrecv.at[h], (nz - 1) * ROWS * 2 * D)
        total = vhalf[h, z].astype(F32)
        for i in range(1, nz):
            total += vzin[h, i - 1].astype(F32)
        dv_out[:, h * 2 * D:(h + 1) * 2 * D] = total.astype(BF16)

    def weight_term(j, vis_t):
        wait_for(krecv.at[j], len(peers) * ROWS * D)
        term = dot(vis_t, kg[j].reshape(nb * ROWS, D), ((1,), (0,)))
        wpart[j] = term.astype(BF16).reshape(nd, per // nd, D)
        for i in range(1, nd):
            t = lax.rem(d + i, nd)
            send(wpart.at[j, t], landed.at[j, i - 1], wrecv.at[j], "dp", t)

    def weight_sum(j):
        wait_for(wrecv.at[j], (nd - 1) * wpart.shape[2] * D)
        total = wpart[j, d].astype(F32)
        for i in range(1, nd):
            total += landed[j, i - 1].astype(F32)
        dw_out[:, j * D:(j + 1) * D] = total

    loads[0].wait()
    loads[1].wait()
    project(0)
    pl.semaphore_wait(barrier, len(line) + nd - 1)
    gather(0)
    for j in range(1, HEADS):
        project(j)
        gather(j)
    forward(0)
    forward(1)
    loads[2].wait()
    loads[3].wait()
    arrive(0)
    attention(0)
    swap(0)
    forward(2)
    forward(3)
    arrive(1)
    exchange()
    attention(1)
    swap(1)
    scatter(0)
    arrive(2)
    attention(2)
    swap(2)
    scatter(1)
    arrive(3)
    attention(3)
    spread(3)
    collect(0)
    scatter(2)
    finish(0)
    finish(1)
    vswap(0)
    collect(1)
    finish(2)
    finish(3)
    vswap(1)
    collect(2)
    wait_for(vrecv, len(peers) * ROWS * per)
    vis_t = vis[...].reshape(nb * ROWS, per).T
    collect_direct(3)
    vscatter(0)
    weight_term(0, vis_t)
    weight_term(1, vis_t)
    vscatter(1)
    weight_term(2, vis_t)
    weight_term(3, vis_t)
    vcollect(0)
    vcollect(1)
    weight_sum(0)
    weight_sum(1)
    weight_sum(2)
    weight_sum(3)
    wait_for(out_sem, sum(sent))


def local(visual_rows, value_matrix, key_weight, queries, output_gradient, visual_len, frame_end):
    nb, nd = lax.axis_size("blk"), lax.axis_size("dp")
    nz = nb // 2
    width = HEADS * D
    features = visual_rows.shape[2]
    per = features // nb
    text = queries.shape[1]
    columns = queries.shape[2]
    dma = pltpu.SemaphoreType.DMA
    smem = pl.BlockSpec(memory_space=pltpu.SMEM)
    vmem = pl.BlockSpec(memory_space=pltpu.VMEM)
    hbm = pl.BlockSpec(memory_space=pltpu.HBM)

    attn_out, query_grad, value_grad, weight_grad = pl.pallas_call(
        kernel,
        out_shape=(
            pltpu.VMEM((text, columns), BF16),
            pltpu.VMEM((text, columns), BF16),
            pltpu.VMEM((ROWS, width), BF16),
            pltpu.VMEM((per // nd, width), F32),
        ),
        in_specs=[smem] * 2 + [hbm] * 5,
        out_specs=(vmem,) * 4,
        scratch_shapes=[
            pltpu.VMEM((ROWS, features), BF16),
            pltpu.VMEM((ROWS, width), BF16),
            pltpu.VMEM((features, width), BF16),
            pltpu.VMEM((text, columns), BF16),
            pltpu.VMEM((text, columns), BF16),
            pltpu.VMEM((nb * ROWS, 2 * D), F32),
            pltpu.VMEM((HEADS, 2, nz, ROWS, 2 * D), BF16),
            pltpu.VMEM((HEADS, nb * ROWS, SPAN), BF16),
            pltpu.VMEM((HEADS, nb * ROWS, SPAN), BF16),
            pltpu.VMEM((HEADS, D, SPAN), BF16),
            pltpu.VMEM((HEADS, 2, nz, ROWS, D), BF16),
            pltpu.VMEM((HEADS, nz, ROWS, D), BF16),
            pltpu.VMEM((HEADS, nz, ROWS, D), BF16),
            pltpu.VMEM((HEADS, nz - 1, ROWS, D), BF16),
            pltpu.VMEM((nb - 1, ROWS, D), BF16),
            pltpu.VMEM((2, 2, nz, ROWS, 2 * D), BF16),
            pltpu.VMEM((2, nz, ROWS, 2 * D), BF16),
            pltpu.VMEM((2, nz, ROWS, 2 * D), BF16),
            pltpu.VMEM((2, nz - 1, ROWS, 2 * D), BF16),
            pltpu.VMEM((HEADS, 2, nz, ROWS, D), BF16),
            pltpu.VMEM((2, nz, ROWS, per), BF16),
            pltpu.VMEM((HEADS, nd, per // nd, D), BF16),
            pltpu.VMEM((HEADS, nd - 1, per // nd, D), BF16),
            dma((4,)), dma((HEADS,)), dma, dma((HEADS, nz - 1)), dma((HEADS,)), dma,
            dma((HEADS,)), dma((HEADS,)), dma, dma((2,)), dma((2,)), dma((HEADS,)), dma((HEADS,)),
        ],
        compiler_params=pltpu.CompilerParams(
            collective_id=0, has_side_effects=True, vmem_limit_bytes=63000 << 10),
        name="cross_attention",
    )(visual_len, frame_end, visual_rows[0], value_matrix[0], key_weight, queries[0], output_gradient[0])
    return attn_out[None], query_grad[None], value_grad[None], weight_grad


def solution(mesh):
    return jax.shard_map(
        local,
        mesh=mesh,
        in_specs=(
            P("dp", "blk", None),
            P("dp", "blk", None),
            P(),
            P("dp", "blk", None),
            P("dp", "blk", None),
            P("dp"),
            P("dp", None),
        ),
        out_specs=(
            P("dp", "blk", None),
            P("dp", "blk", None),
            P("dp", "blk", None),
            P(("blk", "dp"), None),
        ),
        check_vma=False,
    )
```

```python
import math

import jax
import jax.numpy as jnp
from jax import lax
from jax.experimental import pallas as pl
from jax.experimental.pallas import tpu as pltpu
from jax.sharding import PartitionSpec as P

HEADS = 4
GROUP = 8
D = 128
SPAN = GROUP * D
TILE = 128
ROWS = 32
SCALE = D ** (-0.5)
EXP2_SCALE = SCALE * math.log2(math.e)
FILLER = -1e30
MESH = pl.DeviceIdType.MESH
F32 = jnp.float32
BF16 = jnp.bfloat16


def dot(a, b, dims):
    return lax.dot_general(a, b, (dims, ((), ())), preferred_element_type=F32)


def near_first(n):
    return sorted(range(1, n), key=lambda i: min(i, n - i))


def far_first(n):
    return near_first(n)[::-1]


def kernel(length, frames, visual_hbm, values_hbm, weight_hbm, queries_hbm, grads_hbm,
           o_ref, dq_ref, dv_out, dw_out,
           visual, values, weight, q_ref, g_ref, bias,
           kv, w_all, ds_all, o_all, part, yin, half, zin, direct, vpart, vyin, vhalf, vzin,
           kg, vis, wpart, landed,
           load, weight_load, out_sem, zrecv, frecv, vrecv,
           yrecv, hrecv, drecv, vyrecv, vhrecv, kzrecv, krecv, wrecv):
    b = lax.axis_index("blk")
    d = lax.axis_index("dp")
    nb, nd = lax.axis_size("blk"), lax.axis_size("dp")
    nz = nb // 2
    z, y = b // 2, b % 2
    per = visual.shape[1] // nb

    def zmod(i):
        return lax.rem(z + i, nz)

    def zpeer(i):
        return zmod(i) * 2 + y

    partner = b + 1 - 2 * y
    peers = [(i, s) for i in far_first(nz) + [0] for s in (1, 0) if i or s]
    sent = []

    def send(src, dst, rsem, axis, index):
        c = pltpu.make_async_remote_copy(
            src_ref=src, dst_ref=dst, send_sem=out_sem, recv_sem=rsem,
            device_id={axis: index}, device_id_type=MESH)
        c.start()
        sent.append(math.prod(src.shape))
        return c

    def wait_for(sem, elements):
        width = weight.shape[1] if elements % (16 * weight.shape[1]) == 0 else D
        ref = weight.at[pl.ds(0, elements // width), pl.ds(0, width)]
        pltpu.make_async_copy(ref, ref, sem).wait()

    def side(s):
        return y if s == 0 else 1 - y

    def at(i, s):
        return zmod(i) * 2 + side(s)

    loads = []
    for i, (src, dst) in enumerate(((visual_hbm, visual), (values_hbm, values))):
        loads.append(pltpu.make_async_copy(src, dst, load.at[i]))
        loads[-1].start()
    wloads = []
    for j in range(HEADS):
        cols = pl.ds(j * D, D)
        wloads.append(pltpu.make_async_copy(weight_hbm.at[:, cols], weight.at[:, cols], weight_load.at[j]))
        wloads[-1].start()
    for i, (src, dst) in enumerate(((queries_hbm, q_ref), (grads_hbm, g_ref))):
        loads.append(pltpu.make_async_copy(src, dst, load.at[2 + i]))
        loads[-1].start()

    barrier = pltpu.get_barrier_semaphore()
    line = [zpeer(i) for i in range(1, nz)] + [partner]
    for t in line:
        pl.semaphore_signal(barrier, inc=1, device_id={"blk": t}, device_id_type=MESH)
    for i in range(1, nd):
        pl.semaphore_signal(barrier, inc=1, device_id={"dp": lax.rem(d + i, nd)}, device_id_type=MESH)

    limit = jnp.minimum(length[0], TILE * frames[0, b])
    r = lax.broadcasted_iota(jnp.int32, bias.shape, 0)
    row = ((r & (nz * ROWS - 1)) // ROWS) * (2 * ROWS) + (r // (nz * ROWS)) * ROWS + (r & (ROWS - 1))
    bias[...] = jnp.where(row < limit, 0.0, FILLER)

    zcopies, fcopies = {}, {}

    def project(j):
        wloads[j].wait()
        cols = slice(j * D, (j + 1) * D)
        key = jnp.dot(visual[...], weight[:, cols], preferred_element_type=F32)
        kv[j, y, z, :, :D] = key.astype(BF16)
        kv[j, y, z, :, D:] = values[:, cols]

    def gather(j):
        ref = kv.at[j, y, z]
        fcopies[j, 0] = send(ref, ref, frecv.at[j], "blk", partner)
        for i in far_first(nz):
            zcopies[j, i] = send(ref, ref, zrecv.at[j, i - 1], "blk", zpeer(i))

    def forward(j):
        for i in near_first(nz):
            zcopies[j, i].wait_recv()
            ref = kv.at[j, y, zmod(nz - i)]
            fcopies[j, i] = send(ref, ref, frecv.at[j], "blk", partner)

    def arrive(j):
        wait_for(frecv.at[j], nz * ROWS * 2 * D)

    def exchange():
        for i, s in peers:
            t = at(i, s)
            send(visual.at[:, pl.ds(pl.multiple_of(t * per, per), per)], vis.at[y, z], vrecv, "blk", t)
        vis[y, z] = visual[:, pl.ds(pl.multiple_of(b * per, per), per)]

    def stack(ref, j, first, count):
        at0 = j * SPAN + first * D
        return jnp.concatenate([ref[:, at0 + i * D:at0 + (i + 1) * D] for i in range(count)], axis=0)

    def rows_of(j):
        block = kv[j].reshape(nb * ROWS, 2 * D)
        return block[:, :D], block[:, D:]

    def attention(j):
        k, v = rows_of(j)
        v_t = v.T
        for p in range(GROUP // 2):
            cols = slice(2 * p * D, (2 * p + 2) * D)
            q = stack(q_ref, j, 2 * p, 2)
            g_t = stack(g_ref, j, 2 * p, 2).T
            s = dot(k, q, ((1,), (1,))) + bias[...]
            peak = jnp.max(s, axis=0, keepdims=True)
            e = jnp.exp2((s - peak) * EXP2_SCALE)
            probs = e * (1.0 / jnp.sum(e, axis=0, keepdims=True))
            w = probs.astype(BF16)
            w_all[j, :, cols] = w
            o_t = dot(v_t, w, ((1,), (0,))).astype(BF16)
            o_all[j, :, cols] = o_t
            delta = jnp.sum(g_t.astype(F32) * o_t.astype(F32), axis=0, keepdims=True)
            dp = dot(v, g_t, ((1,), (0,)))
            ds_all[j, :, cols] = (probs * ((dp - delta) * SCALE)).astype(BF16)
        dk = dot(ds_all[j], stack(q_ref, j, 0, GROUP), ((1,), (0,)))
        part[j] = dk.astype(BF16).reshape(2, nz, ROWS, D)

    def finish(j):
        k, _ = rows_of(j)
        dv = dot(w_all[j], stack(g_ref, j, 0, GROUP), ((1,), (0,)))
        vpart[j // 2, :, :, :, (j % 2) * D:(j % 2 + 1) * D] = dv.astype(BF16).reshape(2, nz, ROWS, D)
        dq_t = dot(k.T, ds_all[j], ((1,), (0,)))
        for i in range(GROUP):
            cols = slice(j * SPAN + i * D, j * SPAN + (i + 1) * D)
            o_ref[:, cols] = o_all[j, :, i * D:(i + 1) * D].T
            dq_ref[:, cols] = dq_t[:, i * D:(i + 1) * D].T.astype(BF16)

    def swap(j):
        send(part.at[j, 1 - y], yin.at[j], yrecv.at[j], "blk", partner)

    def scatter(j):
        wait_for(yrecv.at[j], nz * ROWS * D)
        half[j] = (part[j, y].astype(F32) + yin[j].astype(F32)).astype(BF16)
        for i in far_first(nz):
            send(half.at[j, zmod(i)], zin.at[j, i - 1], hrecv.at[j], "blk", zpeer(i))

    def publish(j, total):
        kg[j, y, z] = total.astype(BF16)
        ref = kg.at[j, y, z]
        if j == HEADS - 1:
            for i, s in peers:
                send(ref, ref, krecv.at[j], "blk", at(i, s))
        else:
            for i in far_first(nz):
                send(ref, ref, kzrecv.at[j], "blk", zpeer(i))

    def across(j):
        wait_for(kzrecv.at[j], (nz - 1) * ROWS * D)
        ref = kg.at[j, y]
        send(ref, ref, krecv.at[j], "blk", partner)

    def collect(j):
        wait_for(hrecv.at[j], (nz - 1) * ROWS * D)
        total = half[j, z].astype(F32)
        for i in range(1, nz):
            total += zin[j, i - 1].astype(F32)
        publish(j, total)

    def spread(j):
        for n, (i, s) in enumerate(peers):
            send(part.at[j, side(s), zmod(i)], direct.at[n], drecv, "blk", at(i, s))

    def collect_direct(j):
        wait_for(drecv, len(peers) * ROWS * D)
        total = part[j, y, z].astype(F32)
        for n in range(len(peers)):
            total += direct[n].astype(F32)
        publish(j, total)

    def vswap(h):
        send(vpart.at[h, 1 - y], vyin.at[h], vyrecv.at[h], "blk", partner)

    def vscatter(h):
        wait_for(vyrecv.at[h], nz * ROWS * 2 * D)
        vhalf[h] = (vpart[h, y].astype(F32) + vyin[h].astype(F32)).astype(BF16)
        for i in far_first(nz):
            send(vhalf.at[h, zmod(i)], vzin.at[h, i - 1], vhrecv.at[h], "blk", zpeer(i))

    def vcollect(h):
        wait_for(vhrecv.at[h], (nz - 1) * ROWS * 2 * D)
        total = vhalf[h, z].astype(F32)
        for i in range(1, nz):
            total += vzin[h, i - 1].astype(F32)
        dv_out[:, h * 2 * D:(h + 1) * 2 * D] = total.astype(BF16)

    def weight_term(j, vis_t):
        wait_for(krecv.at[j], (len(peers) if j == HEADS - 1 else nz) * ROWS * D)
        term = dot(vis_t, kg[j].reshape(nb * ROWS, D), ((1,), (0,)))
        wpart[j] = term.astype(BF16).reshape(nd, per // nd, D)
        for i in range(1, nd):
            t = lax.rem(d + i, nd)
            send(wpart.at[j, t], landed.at[j, i - 1], wrecv.at[j], "dp", t)

    def weight_sum(j):
        wait_for(wrecv.at[j], (nd - 1) * wpart.shape[2] * D)
        total = wpart[j, d].astype(F32)
        for i in range(1, nd):
            total += landed[j, i - 1].astype(F32)
        dw_out[:, j * D:(j + 1) * D] = total

    loads[0].wait()
    loads[1].wait()
    project(0)
    pl.semaphore_wait(barrier, len(line) + nd - 1)
    gather(0)
    for j in range(1, HEADS):
        project(j)
        gather(j)
    forward(0)
    forward(1)
    loads[2].wait()
    loads[3].wait()
    arrive(0)
    exchange()
    attention(0)
    swap(0)
    forward(2)
    forward(3)
    arrive(1)
    attention(1)
    swap(1)
    scatter(0)
    arrive(2)
    attention(2)
    swap(2)
    scatter(1)
    collect(0)
    arrive(3)
    attention(3)
    spread(3)
    scatter(2)
    finish(0)
    finish(1)
    vswap(0)
    collect(1)
    across(0)
    finish(2)
    finish(3)
    vswap(1)
    collect(2)
    across(1)
    collect_direct(3)
    across(2)
    vscatter(0)
    wait_for(vrecv, len(peers) * ROWS * per)
    vis_t = vis[...].reshape(nb * ROWS, per).T
    weight_term(0, vis_t)
    vscatter(1)
    weight_term(1, vis_t)
    weight_term(2, vis_t)
    weight_term(3, vis_t)
    vcollect(0)
    vcollect(1)
    weight_sum(0)
    weight_sum(1)
    weight_sum(2)
    weight_sum(3)
    wait_for(out_sem, sum(sent))


def local(visual_rows, value_matrix, key_weight, queries, output_gradient, visual_len, frame_end):
    nb, nd = lax.axis_size("blk"), lax.axis_size("dp")
    nz = nb // 2
    width = HEADS * D
    features = visual_rows.shape[2]
    per = features // nb
    text = queries.shape[1]
    columns = queries.shape[2]
    dma = pltpu.SemaphoreType.DMA
    smem = pl.BlockSpec(memory_space=pltpu.SMEM)
    vmem = pl.BlockSpec(memory_space=pltpu.VMEM)
    hbm = pl.BlockSpec(memory_space=pltpu.HBM)

    attn_out, query_grad, value_grad, weight_grad = pl.pallas_call(
        kernel,
        out_shape=(
            pltpu.VMEM((text, columns), BF16),
            pltpu.VMEM((text, columns), BF16),
            pltpu.VMEM((ROWS, width), BF16),
            pltpu.VMEM((per // nd, width), F32),
        ),
        in_specs=[smem] * 2 + [hbm] * 5,
        out_specs=(vmem,) * 4,
        scratch_shapes=[
            pltpu.VMEM((ROWS, features), BF16),
            pltpu.VMEM((ROWS, width), BF16),
            pltpu.VMEM((features, width), BF16),
            pltpu.VMEM((text, columns), BF16),
            pltpu.VMEM((text, columns), BF16),
            pltpu.VMEM((nb * ROWS, 2 * D), F32),
            pltpu.VMEM((HEADS, 2, nz, ROWS, 2 * D), BF16),
            pltpu.VMEM((HEADS, nb * ROWS, SPAN), BF16),
            pltpu.VMEM((HEADS, nb * ROWS, SPAN), BF16),
            pltpu.VMEM((HEADS, D, SPAN), BF16),
            pltpu.VMEM((HEADS, 2, nz, ROWS, D), BF16),
            pltpu.VMEM((HEADS, nz, ROWS, D), BF16),
            pltpu.VMEM((HEADS, nz, ROWS, D), BF16),
            pltpu.VMEM((HEADS, nz - 1, ROWS, D), BF16),
            pltpu.VMEM((nb - 1, ROWS, D), BF16),
            pltpu.VMEM((2, 2, nz, ROWS, 2 * D), BF16),
            pltpu.VMEM((2, nz, ROWS, 2 * D), BF16),
            pltpu.VMEM((2, nz, ROWS, 2 * D), BF16),
            pltpu.VMEM((2, nz - 1, ROWS, 2 * D), BF16),
            pltpu.VMEM((HEADS, 2, nz, ROWS, D), BF16),
            pltpu.VMEM((2, nz, ROWS, per), BF16),
            pltpu.VMEM((HEADS, nd, per // nd, D), BF16),
            pltpu.VMEM((HEADS, nd - 1, per // nd, D), BF16),
            dma((4,)), dma((HEADS,)), dma, dma((HEADS, nz - 1)), dma((HEADS,)), dma,
            dma((HEADS,)), dma((HEADS,)), dma, dma((2,)), dma((2,)), dma((HEADS,)), dma((HEADS,)), dma((HEADS,)),
        ],
        compiler_params=pltpu.CompilerParams(
            collective_id=0, has_side_effects=True, vmem_limit_bytes=63000 << 10),
        name="cross_attention",
    )(visual_len, frame_end, visual_rows[0], value_matrix[0], key_weight, queries[0], output_gradient[0])
    return attn_out[None], query_grad[None], value_grad[None], weight_grad


def solution(mesh):
    return jax.shard_map(
        local,
        mesh=mesh,
        in_specs=(
            P("dp", "blk", None),
            P("dp", "blk", None),
            P(),
            P("dp", "blk", None),
            P("dp", "blk", None),
            P("dp"),
            P("dp", None),
        ),
        out_specs=(
            P("dp", "blk", None),
            P("dp", "blk", None),
            P("dp", "blk", None),
            P(("blk", "dp"), None),
        ),
        check_vma=False,
    )
```
